32 devices in a mesh: ctx: 32 (over z, y, x, core), head: 1.
Axes of the slice: x: 2, y: 2, z: 4, core: 2. Of those that a mesh axis runs over, the one named last changes fastest.
Arguments:
- rotated_queries: bfloat16 [4096, 4096], P('ctx', 'head'), may hold values from -128 to 128
- rotated_keys: bfloat16 [4096, 2048], P('ctx', 'head'), may hold values from -6 to 6
- projected_values: bfloat16 [4096, 2048], P('ctx', 'head'), may hold values from -6 to 6
- doc_ids: int32 [4096], P('ctx'), may hold values from 0 to 15, never falling along the last dimension, each value on 1 to 2048 neighbouring positions
Outputs:
- attended: bfloat16 [4096, 4096], P('ctx', 'head')
The draws below stay inside these ranges and needn't reach their ends.
Inputs may be any that keep to these rules, and one draw needn't show every extreme that they name: `doc_ids`: document numbers never fall along the sequence; each document has 1 to 2048 tokens, one exactly 2048.
All inputs are finite; a program needn't handle non-finite values.
Results may differ from the reference program's by a relative error of at most 0.006.
Values may be sent and summed in bfloat16 or wider, within the bound.
A program may use at most 64 MiB of HBM per device.

```python
import math
import jax
import jax.numpy as jnp
import numpy as np
from jax import lax

QUERY_HEADS = 32
KEY_VALUE_HEADS = 16
HEAD_SIZE = 128
VISIBLE_KEYS = 1024
PRE_SCALAR = 168
SLAB_TOKENS = 128
PACKED_TOKENS = 4096
DOCS = 16
DOC_MOST = 2048


def shared_keys(key):
    slab_start = jnp.clip(jax.random.normal(jax.random.fold_in(key, 11), (PACKED_TOKENS, KEY_VALUE_HEADS * HEAD_SIZE), jnp.float32), -5.0, 5.0)
    return slab_start


def draw_rotated_keys(key, part):
    slab_start = shared_keys(key)
    return slab_start.astype(jnp.bfloat16)


def draw_rotated_queries(key, part):
    fresh = jnp.clip(jax.random.normal(jax.random.fold_in(key, 14), (PACKED_TOKENS, QUERY_HEADS * HEAD_SIZE), jnp.float32), -5.0, 5.0)
    return fresh.astype(jnp.bfloat16)


def block_levels(own_key, shape, split, smallest, largest):
    def one(axis_at, shards_of):
        steps = jax.random.uniform(jax.random.fold_in(jax.random.fold_in(own_key, 6), axis_at), (shards_of,), jnp.float32, smallest / len(split), largest / len(split))
        return jnp.repeat(jnp.exp(steps), shape[axis_at] // shards_of).reshape((-1,) + (1,) * (len(shape) - axis_at - 1))

    factor_of = one(*split[0])
    for cut in split[1:]:
        factor_of = factor_of * one(*cut)
    return factor_of


def length_profile(amount, total, bound, skew):
    portions = [(1 << 20) // math.isqrt(standing ** skew) + 1 for standing in range(2, amount + 1)]
    rest, given = total - bound - (amount - 1), [1] * (amount - 1)
    while rest > 0:
        free = [i for i in range(amount - 1) if given[i] < bound]
        mass, left = sum([portions[i] for i in free]), rest
        for i in free:
            extra = min(bound - given[i], max(1, left * portions[i] // mass), rest)
            given[i] = given[i] + extra
            rest = rest - extra
    return np.array([bound] + given)


def ragged_sizes(stream_key, number_of, total, bound, lean):
    if number_of == 2:
        one = jax.random.randint(stream_key, (), max(1, total - bound), min(bound, total - 1) + 1)
        return jnp.stack([one, total - one])
    sizes = jnp.asarray(length_profile(number_of, total, bound, lean), jnp.int32)
    pairs = (number_of - 1) // 2
    donor, sink = sizes[1:1 + 2 * pairs:2], sizes[2:2 + 2 * pairs:2]
    room = jnp.minimum(donor - 1, bound - sink)
    shifted = jax.random.randint(jax.random.fold_in(stream_key, 1), (pairs,), 0, 1 << 20) % (room + 1)
    sizes = sizes.at[1:1 + 2 * pairs:2].set(donor - shifted).at[2:2 + 2 * pairs:2].set(sink + shifted)
    return sizes[jax.random.permutation(jax.random.fold_in(stream_key, 2), number_of)]


def normal_values(rng, extent, spread, most, pieces=(), kind=jnp.bfloat16):
    drawn = spread * jax.random.normal(rng, extent, jnp.float32)
    if pieces:
        drawn = drawn * block_levels(rng, extent, pieces, -0.22, 0.18)
    return jnp.clip(drawn, -most, most).astype(kind)


def setup_inputs(seed: int = 0) -> dict:
    keys = jax.random.split(jax.random.key(seed), 5)
    rotated_queries = draw_rotated_queries(jax.random.fold_in(keys[4], 71), 0)
    rotated_keys = draw_rotated_keys(jax.random.fold_in(keys[4], 71), 0)
    projected_values = normal_values(keys[2], (PACKED_TOKENS, KEY_VALUE_HEADS * HEAD_SIZE), 1.0, 6.0, ((0, 32),))
    doc_ids = jnp.searchsorted(jnp.cumsum(ragged_sizes(keys[3], DOCS, PACKED_TOKENS, DOC_MOST, 2)), jnp.arange(PACKED_TOKENS), side="right").astype(jnp.int32)
    return dict(rotated_queries=rotated_queries, rotated_keys=rotated_keys, projected_values=projected_values, doc_ids=doc_ids)


def reference(rotated_queries, rotated_keys, projected_values, doc_ids):
    query_group = QUERY_HEADS // KEY_VALUE_HEADS
    scale = PRE_SCALAR ** -0.5
    blocks = PACKED_TOKENS // SLAB_TOKENS
    padded_keys = jnp.concatenate([jnp.zeros((VISIBLE_KEYS, KEY_VALUE_HEADS * HEAD_SIZE), rotated_keys.dtype), rotated_keys], axis=0)
    padded_values = jnp.concatenate([jnp.zeros((VISIBLE_KEYS, KEY_VALUE_HEADS * HEAD_SIZE), projected_values.dtype), projected_values], axis=0)
    ids_pad = jnp.concatenate([jnp.full((VISIBLE_KEYS,), -1, jnp.int32), doc_ids.astype(jnp.int32)], axis=0)
    span_length = VISIBLE_KEYS + SLAB_TOKENS

    def one_block(block):
        first_position = (block * SLAB_TOKENS).astype(jnp.int32)
        query_rows = lax.dynamic_slice_in_dim(rotated_queries, first_position, SLAB_TOKENS, 0).reshape(SLAB_TOKENS, KEY_VALUE_HEADS, query_group, HEAD_SIZE)
        q_ids = lax.dynamic_slice_in_dim(doc_ids.astype(jnp.int32), first_position, SLAB_TOKENS, 0)
        key_rows = lax.dynamic_slice_in_dim(padded_keys, first_position, span_length, 0).reshape(span_length, KEY_VALUE_HEADS, HEAD_SIZE)
        value_rows = lax.dynamic_slice_in_dim(padded_values, first_position, span_length, 0).reshape(span_length, KEY_VALUE_HEADS, HEAD_SIZE)
        k_ids = lax.dynamic_slice_in_dim(ids_pad, first_position, span_length, 0)
        q_pos = first_position + jnp.arange(SLAB_TOKENS, dtype=jnp.int32)
        k_pos = first_position - VISIBLE_KEYS + jnp.arange(span_length, dtype=jnp.int32)
        mask = (k_ids[None, :] == q_ids[:, None]) & (k_pos[None, :] <= q_pos[:, None]) & (q_pos[:, None] - k_pos[None, :] < VISIBLE_KEYS) & (k_pos[None, :] >= 0)
        scores = jnp.einsum("tgrd,lgd->grtl", query_rows.astype(jnp.float32), key_rows.astype(jnp.float32)) * scale
        masked = jnp.where(mask, scores, jnp.float32(-1e30))
        top = jnp.max(masked, axis=-1, keepdims=True)
        weights = jnp.where(mask, jnp.exp(masked - top), jnp.float32(0.0))
        total = jnp.sum(weights, axis=-1)
        rounded = weights.astype(jnp.bfloat16)
        accum = jnp.einsum("grtl,lgd->grtd", rounded.astype(jnp.float32), value_rows.astype(jnp.float32))
        out = accum / total[..., None]
        return jnp.transpose(out, (2, 0, 1, 3)).reshape(SLAB_TOKENS, QUERY_HEADS * HEAD_SIZE).astype(jnp.bfloat16)

    outs = lax.map(one_block, jnp.arange(blocks, dtype=jnp.int32))
    return outs.reshape(PACKED_TOKENS, QUERY_HEADS * HEAD_SIZE)
```

```python
import functools
import math

import jax
import jax.numpy as jnp
from jax import lax
from jax.experimental import pallas as pl
from jax.experimental.pallas import tpu as pltpu
from jax.sharding import PartitionSpec as P

HEAD_SIZE = 128
VISIBLE_KEYS = 1024
PRE_SCALAR = 168
CHUNK_HEADS = 2
MESH = pl.DeviceIdType.MESH


def kernel(
    n,
    group,
    q_hbm,
    k_hbm,
    v_hbm,
    ids_hbm,
    o_hbm,
    kv,
    ids,
    q_buf,
    o_buf,
    bias,
    send_sem,
    recv_sem,
    ids_send_sem,
    ids_recv_sem,
    own_sem,
    q_sem,
    ids_sem,
    out_sem,
):
    rows = q_hbm.shape[0]
    width = k_hbm.shape[1]
    span = VISIBLE_KEYS // rows
    keys = VISIBLE_KEYS + rows
    chips = span // 2
    cols = CHUNK_HEADS * HEAD_SIZE
    chunks = width // cols
    q_cols = cols * group
    direct = chips
    me = lax.axis_index("ctx")
    local = lax.rem(me, span)
    base = me - local
    chip = local // 2
    core = lax.rem(local, 2)
    sib = 2 * chip + 1 - core
    z_next = lax.rem(me + span, n)
    z_prev = lax.rem(me + n - span, n)

    def back(dst, src):
        return lax.rem(dst - src + span, span)

    def place(steps):
        return pl.multiple_of((span - steps) * rows, rows)

    def block(steps, chunk):
        start = pl.multiple_of(chunk * cols, cols)
        return kv.at[:, pl.ds(place(steps), rows), pl.ds(start, cols)]

    def copy(src, dst, target, kind, chunk):
        return pltpu.make_async_remote_copy(
            src_ref=block(src, chunk),
            dst_ref=block(dst, chunk),
            send_sem=send_sem.at[kind, chunk],
            recv_sem=recv_sem.at[dst, chunk],
            device_id={"ctx": target},
            device_id_type=MESH,
        )

    def ids_copy(src, dst, target, kind, chunk):
        return pltpu.make_async_remote_copy(
            src_ref=ids.at[src],
            dst_ref=ids.at[dst],
            send_sem=ids_send_sem.at[kind],
            recv_sem=ids_recv_sem.at[dst],
            device_id={"ctx": target},
            device_id_type=MESH,
        )

    def other(turn):
        return lax.rem(chip + turn, chips)

    def send_own(copy, chunk):
        copy(0, span, z_next, 0, chunk).start()
        for turn in range(1, chips):
            to = 2 * other(turn) + core

            @pl.when(to > local)
            def _():
                copy(0, back(to, local), base + to, turn, chunk).start()

        @pl.when(core == 0)
        def _():
            copy(0, back(sib, local), base + sib, direct, chunk).start()

    def send_past(copy, chunk):
        copy(0, span, z_next, 0, chunk).wait_recv()
        for turn in range(1, chips):
            to = 2 * other(turn) + core

            @pl.when(to < local)
            def _():
                copy(span, back(to, local), base + to, turn, chunk).start()

        @pl.when(core == 1)
        def _():
            copy(span, back(sib, local), base + sib, direct, chunk).start()

    def relay(copy, chunk):
        for turn in range(1, chips):
            source = 2 * other(turn) + core
            here = back(local, source)
            copy(0, here, z_next, 0, chunk).wait_recv()
            copy(here, back(sib, source), base + sib, direct + turn, chunk).start()

    def gather(copy, chunk):
        copy(0, back(local, sib), z_next, 0, chunk).wait_recv()
        for turn in range(1, chips):
            source = 2 * other(turn) + 1 - core
            copy(0, back(local, source), z_next, 0, chunk).wait_recv()

    def own_copies(chunk):
        start = pl.multiple_of(chunk * cols, cols)
        return [
            pltpu.make_async_copy(
                ref.at[:, pl.ds(start, cols)],
                kv.at[which, pl.ds(VISIBLE_KEYS, rows), pl.ds(start, cols)],
                own_sem.at[which, chunk],
            )
            for which, ref in enumerate((k_hbm, v_hbm))
        ]

    q_copy = pltpu.make_async_copy(q_hbm, q_buf, q_sem)
    own_ids = pltpu.make_async_copy(ids_hbm, ids.at[0], ids_sem)

    def out_copy(chunk):
        part = pl.ds(pl.multiple_of(chunk * q_cols, q_cols), q_cols)
        return pltpu.make_async_copy(o_buf.at[:, part], o_hbm.at[:, part], out_sem.at[chunk])

    own_ids.start()

    def fetch(chunk, _):
        for c in own_copies(chunk):
            c.start()
        return 0

    lax.fori_loop(0, chunks, fetch, 0)
    q_copy.start()

    barrier = pltpu.get_barrier_semaphore()
    partners = [z_next, z_prev, base + sib] + [
        base + 2 * other(turn) + core for turn in range(1, chips)
    ]
    for partner in partners:
        pl.semaphore_signal(barrier, inc=1, device_id={"ctx": partner}, device_id_type=MESH)
    pl.semaphore_wait(barrier, len(partners))

    own_ids.wait()
    send_own(ids_copy, 0)

    def start_own(chunk, _):
        for c in own_copies(chunk):
            c.wait()
        send_own(copy, chunk)
        return 0

    lax.fori_loop(0, chunks, start_own, 0)

    send_past(ids_copy, 0)
    send_past(copy, 0)
    relay(ids_copy, 0)
    send_past(copy, 1)
    relay(copy, 0)
    gather(ids_copy, 0)

    own_row = ids[0].astype(jnp.float32)
    query_ids = jnp.broadcast_to(own_row, (rows, rows)).T
    row = lax.broadcasted_iota(jnp.int32, (rows, rows), 0)
    column = lax.broadcasted_iota(jnp.int32, (rows, rows), 1)
    for steps in range(span, -1, -1):
        seen = query_ids == ids[steps].astype(jnp.float32)
        key_pos = (me - steps) * rows + column
        query_pos = me * rows + row
        seen = seen & (key_pos >= 0) & (key_pos <= query_pos)
        seen = seen & (query_pos - key_pos < VISIBLE_KEYS)
        bias[:, (span - steps) * rows : (span - steps + 1) * rows] = jnp.where(
            seen, jnp.float32(0.0), jnp.float32(-1e30)
        )
    q_copy.wait()
    factor = PRE_SCALAR ** (-0.5) * math.log2(math.e)

    def step(chunk, _):
        @pl.when(chunk + 2 < chunks)
        def _():
            send_past(copy, chunk + 2)

        @pl.when(chunk + 1 < chunks)
        def _():
            relay(copy, chunk + 1)

        gather(copy, chunk)
        for head in range(CHUNK_HEADS):
            at = pl.multiple_of(chunk * cols + head * HEAD_SIZE, HEAD_SIZE)
            key_rows = kv[0, :, pl.ds(at, HEAD_SIZE)]
            values = kv[1, :, pl.ds(at, HEAD_SIZE)]
            weights, totals = [], []
            queries = jnp.concatenate(
                [
                    q_buf[:, pl.ds(pl.multiple_of(at * group + g * HEAD_SIZE, HEAD_SIZE), HEAD_SIZE)]
                    for g in range(group)
                ],
                axis=0,
            )
            scores = lax.dot_general(
                queries, key_rows, (((1,), (1,)), ((), ())), preferred_element_type=jnp.float32
            )
            for g in range(group):
                masked = scores[g * rows : (g + 1) * rows] + bias[...]
                top = jnp.max(masked, axis=1, keepdims=True)
                weight = jnp.exp2((masked - top) * factor)
                totals.append(jnp.sum(weight, axis=1, keepdims=True))
                weights.append(weight.astype(jnp.bfloat16))
            summed = jnp.dot(
                jnp.concatenate(weights, axis=0), values, preferred_element_type=jnp.float32
            )
            for g in range(group):
                to = pl.multiple_of(at * group + g * HEAD_SIZE, HEAD_SIZE)
                o_buf[:, pl.ds(to, HEAD_SIZE)] = (
                    summed[g * rows : (g + 1) * rows] / totals[g]
                ).astype(jnp.bfloat16)
        out_copy(chunk).start()
        return 0

    lax.fori_loop(0, chunks, step, 0)

    def finish(chunk, _):
        for kind in range(2 * chips):
            copy(0, span, z_next, kind, chunk).wait_send()
        out_copy(chunk).wait()
        return 0

    lax.fori_loop(0, chunks, finish, 0)
    for kind in range(2 * chips):
        ids_copy(0, span, z_next, kind, 0).wait_send()


def per_device(n, rotated_queries, rotated_keys, projected_values, doc_ids):
    rows, q_width = rotated_queries.shape
    width = rotated_keys.shape[1]
    span = VISIBLE_KEYS // rows
    chunks = width // (CHUNK_HEADS * HEAD_SIZE)
    keys = VISIBLE_KEYS + rows
    dma = pltpu.SemaphoreType.DMA
    return pl.pallas_call(
        functools.partial(kernel, n, q_width // width),
        out_shape=jax.ShapeDtypeStruct((rows, q_width), jnp.bfloat16),
        in_specs=[pl.BlockSpec(memory_space=pl.ANY)] * 4,
        out_specs=pl.BlockSpec(memory_space=pl.ANY),
        scratch_shapes=[
            pltpu.VMEM((2, keys, width), jnp.bfloat16),
            pltpu.VMEM((span + 1, 1, rows), jnp.int32),
            pltpu.VMEM((rows, q_width), jnp.bfloat16),
            pltpu.VMEM((rows, q_width), jnp.bfloat16),
            pltpu.VMEM((rows, keys), jnp.float32),
            dma((span, chunks)),
            dma((span + 1, chunks)),
            dma((span,)),
            dma((span + 1,)),
            dma((2, chunks)),
            dma,
            dma,
            dma((chunks,)),
        ],
        compiler_params=pltpu.CompilerParams(collective_id=0, has_side_effects=True),
    )(rotated_queries, rotated_keys, projected_values, doc_ids.reshape(1, rows))


def solution(mesh):
    in_specs = (P("ctx", "head"), P("ctx", "head"), P("ctx", "head"), P("ctx"))
    return jax.shard_map(
        functools.partial(per_device, mesh.shape["ctx"]),
        mesh=mesh,
        in_specs=in_specs,
        out_specs=P("ctx", "head"),
        check_vma=False,
    )
```

```python
import functools
import math

import jax
import jax.numpy as jnp
from jax import lax
from jax.experimental import pallas as pl
from jax.experimental.pallas import tpu as pltpu
from jax.sharding import PartitionSpec as P

HEAD_SIZE = 128
VISIBLE_KEYS = 1024
PRE_SCALAR = 168
CHUNK_HEADS = 2
AHEAD = 0
MESH = pl.DeviceIdType.MESH


def kernel(
    n,
    group,
    q_hbm,
    k_hbm,
    v_hbm,
    ids_hbm,
    o_hbm,
    kv,
    ids,
    q_buf,
    o_buf,
    bias,
    send_sem,
    recv_sem,
    ids_send_sem,
    ids_recv_sem,
    own_sem,
    q_sem,
    ids_sem,
    out_sem,
):
    rows = q_hbm.shape[0]
    width = k_hbm.shape[1]
    span = VISIBLE_KEYS // rows
    keys = VISIBLE_KEYS + rows
    chips = span // 2
    cols = CHUNK_HEADS * HEAD_SIZE
    chunks = width // cols
    q_cols = cols * group
    me = lax.axis_index("ctx")
    local = lax.rem(me, span)
    base = me - local
    chip = local // 2
    core = lax.rem(local, 2)
    sib = 2 * chip + 1 - core
    z_next = lax.rem(me + span, n)
    z_prev = lax.rem(me + n - span, n)

    def back(dst, src):
        return lax.rem(dst - src + span, span)

    def block(steps, chunk):
        return kv.at[chunk, span - steps]

    def copy(src, dst, target, kind, chunk):
        return pltpu.make_async_remote_copy(
            src_ref=block(src, chunk),
            dst_ref=block(dst, chunk),
            send_sem=send_sem.at[kind, chunk],
            recv_sem=recv_sem.at[dst, chunk],
            device_id={"ctx": target},
            device_id_type=MESH,
        )

    def ids_copy(src, dst, target, kind, chunk):
        return pltpu.make_async_remote_copy(
            src_ref=ids.at[src],
            dst_ref=ids.at[dst],
            send_sem=ids_send_sem.at[kind],
            recv_sem=ids_recv_sem.at[dst],
            device_id={"ctx": target},
            device_id_type=MESH,
        )

    beside = chip + 1 - 2 * lax.rem(chip, 2)
    across = lax.rem(chip + 2, chips)
    far = 3 - chip

    def corner(source):
        return lax.rem(source, 3) == 0

    def by_across(source, chunk):
        third = lax.rem(chunk, 3)
        return jnp.logical_or(
            jnp.logical_and(corner(source), third == 1),
            jnp.logical_and(jnp.logical_not(corner(source)), third != 0),
        )

    def by_beside(source, chunk):
        return jnp.logical_and(corner(source), jnp.logical_not(by_across(source, chunk)))

    def straight(source, chunk):
        return jnp.logical_not(jnp.logical_or(corner(source), by_across(source, chunk)))

    def onward(copy, chunk):
        copy(0, span, z_next, 0, chunk).start()

    def send(copy, chunk, steps, chosen):
        for kind, there in ((1, beside), (2, across), (3, far)):
            to = 2 * there + core
            wanted = chosen(to)
            if kind == 3:
                wanted = jnp.logical_and(wanted, straight(chip, chunk))

            @pl.when(wanted)
            def _():
                copy(steps, back(to, local), base + to, kind, chunk).start()

        @pl.when(chosen(sib))
        def _():
            copy(steps, back(sib, local), base + sib, 4, chunk).start()

    def send_own(copy, chunk):
        send(copy, chunk, 0, lambda to: to > local)

    def send_past(copy, chunk):
        copy(0, span, z_next, 0, chunk).wait_recv()
        send(copy, chunk, span, lambda to: to < local)

    def to_sib(copy, chunk, there, kind):
        source = 2 * there + core
        copy(back(local, source), back(sib, source), base + sib, kind, chunk).start()

    def arrive(copy, chunk, there):
        copy(0, back(local, 2 * there + core), z_next, 0, chunk).wait_recv()

    def relay_near(copy, chunk):
        for kind, there, target, chosen in (
            (8, across, beside, by_across),
            (9, beside, across, by_beside),
        ):
            arrive(copy, chunk, there)
            source, to = 2 * there + core, 2 * target + core

            @pl.when(chosen(there, chunk))
            def _():
                copy(back(local, source), back(to, source), base + to, kind, chunk).start()

            to_sib(copy, chunk, there, kind - 3)

    def relay_far(copy, chunk):
        arrive(copy, chunk, far)
        to_sib(copy, chunk, far, 7)

    def gather(copy, chunk):
        copy(0, back(local, sib), z_next, 0, chunk).wait_recv()
        for there in (beside, across, far):
            copy(0, back(local, 2 * there + 1 - core), z_next, 0, chunk).wait_recv()

    def sent(copy, chunk):
        for kind in (0, 1, 2, 4, 5, 6, 7):
            copy(0, span, z_next, kind, chunk).wait_send()
        for kind, wanted in (
            (3, straight(chip, chunk)),
            (8, by_across(across, chunk)),
            (9, by_beside(beside, chunk)),
        ):

            @pl.when(wanted)
            def _():
                copy(0, span, z_next, kind, chunk).wait_send()

    def own_copies(chunk):
        start = pl.multiple_of(chunk * cols, cols)
        return [
            pltpu.make_async_copy(
                ref.at[:, pl.ds(start, cols)],
                kv.at[chunk, span, which],
                own_sem.at[which, chunk],
            )
            for which, ref in enumerate((k_hbm, v_hbm))
        ]

    q_copy = pltpu.make_async_copy(q_hbm, q_buf, q_sem)
    own_ids = pltpu.make_async_copy(ids_hbm, ids.at[0], ids_sem)

    def out_copy(chunk):
        part = pl.ds(pl.multiple_of(chunk * q_cols, q_cols), q_cols)
        return pltpu.make_async_copy(o_buf.at[:, part], o_hbm.at[:, part], out_sem.at[chunk])

    own_ids.start()

    def fetch(chunk, _):
        for c in own_copies(chunk):
            c.start()
        return 0

    lax.fori_loop(0, chunks, fetch, 0)
    q_copy.start()

    barrier = pltpu.get_barrier_semaphore()
    partners = [z_next, z_prev, base + sib] + [
        base + 2 * there + core for there in (beside, across, far)
    ]
    for partner in partners:
        pl.semaphore_signal(barrier, inc=1, device_id={"ctx": partner}, device_id_type=MESH)
    pl.semaphore_wait(barrier, len(partners))

    own_ids.wait()
    onward(ids_copy, 0)

    def start_own(chunk, _):
        for c in own_copies(chunk):
            c.wait()
        onward(copy, chunk)
        return 0

    lax.fori_loop(0, 1, start_own, 0)
    send_own(ids_copy, 0)
    send_own(copy, 0)
    lax.fori_loop(1, min(AHEAD + 4, chunks), start_own, 0)

    def ahead(chunk, _):
        send_own(copy, chunk)
        return 0

    lax.fori_loop(1, min(AHEAD + 3, chunks), ahead, 0)

    send_past(ids_copy, 0)
    send_past(copy, 0)
    relay_near(ids_copy, 0)
    send_past(copy, 1)
    relay_near(copy, 0)
    relay_far(ids_copy, 0)
    send_past(copy, 2)
    relay_near(copy, 1)
    relay_far(copy, 0)
    gather(ids_copy, 0)

    own_row = ids[0].astype(jnp.float32)
    query_ids = jnp.broadcast_to(own_row, (rows, rows)).T
    row = lax.broadcasted_iota(jnp.int32, (rows, rows), 0)
    column = lax.broadcasted_iota(jnp.int32, (rows, rows), 1)
    for steps in range(span, -1, -1):
        seen = query_ids == ids[steps].astype(jnp.float32)
        key_pos = (me - steps) * rows + column
        query_pos = me * rows + row
        seen = seen & (key_pos >= 0) & (key_pos <= query_pos)
        seen = seen & (query_pos - key_pos < VISIBLE_KEYS)
        bias[:, (span - steps) * rows : (span - steps + 1) * rows] = jnp.where(
            seen, jnp.float32(0.0), jnp.float32(-1e30)
        )
    q_copy.wait()
    factor = PRE_SCALAR ** (-0.5) * math.log2(math.e)

    def step(chunk, _):
        @pl.when(chunk + AHEAD + 4 < chunks)
        def _():
            start_own(chunk + AHEAD + 4, 0)

        for later, act in (
            (3 + AHEAD, send_own),
            (3, send_past),
            (2, relay_near),
            (1, relay_far),
        ):

            @pl.when(chunk + later < chunks)
            def _():
                act(copy, chunk + later)

        gather(copy, chunk)
        for head in range(CHUNK_HEADS):
            at = pl.multiple_of(chunk * cols + head * HEAD_SIZE, HEAD_SIZE)
            lanes = slice(head * HEAD_SIZE, (head + 1) * HEAD_SIZE)
            key_rows = kv[chunk, :, 0, :, lanes].reshape(keys, HEAD_SIZE)
            values = kv[chunk, :, 1, :, lanes].reshape(keys, HEAD_SIZE)
            weights, totals = [], []
            queries = jnp.concatenate(
                [
                    q_buf[:, pl.ds(pl.multiple_of(at * group + g * HEAD_SIZE, HEAD_SIZE), HEAD_SIZE)]
                    for g in range(group)
                ],
                axis=0,
            )
            scores = lax.dot_general(
                queries, key_rows, (((1,), (1,)), ((), ())), preferred_element_type=jnp.float32
            )
            for g in range(group):
                masked = scores[g * rows : (g + 1) * rows] + bias[...]
                top = jnp.max(masked, axis=1, keepdims=True)
                weight = jnp.exp2((masked - top) * factor)
                totals.append(jnp.sum(weight, axis=1, keepdims=True))
                weights.append(weight.astype(jnp.bfloat16))
            summed = jnp.dot(
                jnp.concatenate(weights, axis=0), values, preferred_element_type=jnp.float32
            )
            for g in range(group):
                to = pl.multiple_of(at * group + g * HEAD_SIZE, HEAD_SIZE)
                o_buf[:, pl.ds(to, HEAD_SIZE)] = (
                    summed[g * rows : (g + 1) * rows] / totals[g]
                ).astype(jnp.bfloat16)
        out_copy(chunk).start()
        return 0

    lax.fori_loop(0, chunks, step, 0)

    def finish(chunk, _):
        sent(copy, chunk)
        out_copy(chunk).wait()
        return 0

    lax.fori_loop(0, chunks, finish, 0)
    sent(ids_copy, 0)


def per_device(n, rotated_queries, rotated_keys, projected_values, doc_ids):
    rows, q_width = rotated_queries.shape
    width = rotated_keys.shape[1]
    span = VISIBLE_KEYS // rows
    chunks = width // (CHUNK_HEADS * HEAD_SIZE)
    keys = VISIBLE_KEYS + rows
    dma = pltpu.SemaphoreType.DMA
    return pl.pallas_call(
        functools.partial(kernel, n, q_width // width),
        out_shape=jax.ShapeDtypeStruct((rows, q_width), jnp.bfloat16),
        in_specs=[pl.BlockSpec(memory_space=pl.ANY)] * 4,
        out_specs=pl.BlockSpec(memory_space=pl.ANY),
        scratch_shapes=[
            pltpu.VMEM((chunks, span + 1, 2, rows, width // chunks), jnp.bfloat16),
            pltpu.VMEM((span + 1, 1, rows), jnp.int32),
            pltpu.VMEM((rows, q_width), jnp.bfloat16),
            pltpu.VMEM((rows, q_width), jnp.bfloat16),
            pltpu.VMEM((rows, keys), jnp.float32),
            dma((10, chunks)),
            dma((span + 1, chunks)),
            dma((10,)),
            dma((span + 1,)),
            dma((2, chunks)),
            dma,
            dma,
            dma((chunks,)),
        ],
        compiler_params=pltpu.CompilerParams(collective_id=0, has_side_effects=True),
    )(rotated_queries, rotated_keys, projected_values, doc_ids.reshape(1, rows))


def solution(mesh):
    in_specs = (P("ctx", "head"), P("ctx", "head"), P("ctx", "head"), P("ctx"))
    return jax.shard_map(
        functools.partial(per_device, mesh.shape["ctx"]),
        mesh=mesh,
        in_specs=in_specs,
        out_specs=P("ctx", "head"),
        check_vma=False,
    )
```

```python
import functools
import math

import jax
import jax.numpy as jnp
from jax import lax
from jax.experimental import pallas as pl
from jax.experimental.pallas import tpu as pltpu
from jax.sharding import PartitionSpec as P

HEAD_SIZE = 128
VISIBLE_KEYS = 1024
PRE_SCALAR = 168
CHUNK_HEADS = 1
AHEAD = 0
PAST = 6
NEAR = 4
FAR = 2
MESH = pl.DeviceIdType.MESH


def kernel(
    n,
    group,
    q_hbm,
    k_hbm,
    v_hbm,
    ids_hbm,
    o_hbm,
    kv,
    ids,
    q_buf,
    o_buf,
    bias,
    send_sem,
    recv_sem,
    ids_send_sem,
    ids_recv_sem,
    own_sem,
    q_sem,
    ids_sem,
    out_sem,
    stand_sem,
    ids_stand_sem,
):
    rows = q_hbm.shape[0]
    width = k_hbm.shape[1]
    span = VISIBLE_KEYS // rows
    keys = VISIBLE_KEYS + rows
    chips = span // 2
    cols = CHUNK_HEADS * HEAD_SIZE
    chunks = width // cols
    q_cols = cols * group
    me = lax.axis_index("ctx")
    local = lax.rem(me, span)
    base = me - local
    chip = local // 2
    core = lax.rem(local, 2)
    sib = 2 * chip + 1 - core
    z_next = lax.rem(me + span, n)
    z_prev = lax.rem(me + n - span, n)

    def back(dst, src):
        return lax.rem(dst - src + span, span)

    def block(steps, chunk):
        return kv.at[chunk, span - steps]

    def copy(src, dst, target, kind, chunk):
        return pltpu.make_async_remote_copy(
            src_ref=block(src, chunk),
            dst_ref=block(dst, chunk),
            send_sem=send_sem.at[kind, chunk],
            recv_sem=recv_sem.at[dst, chunk],
            device_id={"ctx": target},
            device_id_type=MESH,
        )

    def ids_copy(src, dst, target, kind, chunk):
        return pltpu.make_async_remote_copy(
            src_ref=ids.at[src],
            dst_ref=ids.at[dst],
            send_sem=ids_send_sem.at[kind],
            recv_sem=ids_recv_sem.at[dst],
            device_id={"ctx": target},
            device_id_type=MESH,
        )

    beside = chip + 1 - 2 * lax.rem(chip, 2)
    across = lax.rem(chip + 2, chips)
    far = 3 - chip

    def corner(source):
        return lax.rem(source, 3) == 0

    def by_across(source, chunk):
        third = lax.rem(chunk, 3)
        return jnp.logical_or(
            jnp.logical_and(corner(source), third == 1),
            jnp.logical_and(jnp.logical_not(corner(source)), third != 0),
        )

    def by_beside(source, chunk):
        return jnp.logical_and(corner(source), jnp.logical_not(by_across(source, chunk)))

    def straight(source, chunk):
        return jnp.logical_not(jnp.logical_or(corner(source), by_across(source, chunk)))

    def stand_in(chunk):
        start = pl.multiple_of(chunk * cols, cols)
        return [
            pltpu.make_async_copy(
                ref.at[:, pl.ds(start, cols)], kv.at[chunk, 0, which], stand_sem.at[which, chunk]
            )
            for which, ref in enumerate((k_hbm, v_hbm))
        ]

    ids_stand = pltpu.make_async_copy(ids_hbm, ids.at[span], ids_stand_sem)

    def onward(copy, chunk):
        @pl.when(me + span < n)
        def _():
            copy(0, span, z_next, 0, chunk).start()

    def past_here(copy, chunk):
        @pl.when(me >= span)
        def _():
            copy(0, span, z_next, 0, chunk).wait_recv()

        @pl.when(me < span)
        def _():
            for c in [ids_stand] if copy is ids_copy else stand_in(chunk):
                c.wait()

    def send(copy, chunk, steps, chosen):
        for kind, there in ((1, beside), (2, across), (3, far)):
            to = 2 * there + core
            wanted = chosen(to)
            if kind == 3:
                wanted = jnp.logical_and(wanted, straight(chip, chunk))

            @pl.when(wanted)
            def _():
                copy(steps, back(to, local), base + to, kind, chunk).start()

        @pl.when(chosen(sib))
        def _():
            copy(steps, back(sib, local), base + sib, 4, chunk).start()

    def send_own(copy, chunk):
        send(copy, chunk, 0, lambda to: to > local)

    def send_past(copy, chunk):
        past_here(copy, chunk)
        send(copy, chunk, span, lambda to: to < local)

    def to_sib(copy, chunk, there, kind):
        source = 2 * there + core
        copy(back(local, source), back(sib, source), base + sib, kind, chunk).start()

    def arrive(copy, chunk, there):
        copy(0, back(local, 2 * there + core), z_next, 0, chunk).wait_recv()

    def relay_near(copy, chunk):
        for kind, there, target, chosen in (
            (8, across, beside, by_across),
            (9, beside, across, by_beside),
        ):
            arrive(copy, chunk, there)
            source, to = 2 * there + core, 2 * target + core

            @pl.when(chosen(there, chunk))
            def _():
                copy(back(local, source), back(to, source), base + to, kind, chunk).start()

            to_sib(copy, chunk, there, kind - 3)

    def relay_far(copy, chunk):
        arrive(copy, chunk, far)
        to_sib(copy, chunk, far, 7)

    def gather(copy, chunk):
        copy(0, back(local, sib), z_next, 0, chunk).wait_recv()
        for there in (beside, across, far):
            copy(0, back(local, 2 * there + 1 - core), z_next, 0, chunk).wait_recv()

    def sent(copy, chunk):
        for kind in (1, 2, 4, 5, 6, 7):
            copy(0, span, z_next, kind, chunk).wait_send()
        for kind, wanted in (
            (0, me + span < n),
            (3, straight(chip, chunk)),
            (8, by_across(across, chunk)),
            (9, by_beside(beside, chunk)),
        ):

            @pl.when(wanted)
            def _():
                copy(0, span, z_next, kind, chunk).wait_send()

    def own_copies(chunk):
        start = pl.multiple_of(chunk * cols, cols)
        return [
            pltpu.make_async_copy(
                ref.at[:, pl.ds(start, cols)],
                kv.at[chunk, span, which],
                own_sem.at[which, chunk],
            )
            for which, ref in enumerate((k_hbm, v_hbm))
        ]

    q_copy = pltpu.make_async_copy(q_hbm, q_buf, q_sem)
    own_ids = pltpu.make_async_copy(ids_hbm, ids.at[0], ids_sem)

    def out_copy(chunk):
        part = pl.ds(pl.multiple_of(chunk * q_cols, q_cols), q_cols)
        return pltpu.make_async_copy(o_buf.at[:, part], o_hbm.at[:, part], out_sem.at[chunk])

    own_ids.start()

    @pl.when(me < span)
    def _():
        ids_stand.start()

    def fetch(chunk, _):
        for c in own_copies(chunk):
            c.start()

        @pl.when(me < span)
        def _():
            for c in stand_in(chunk):
                c.start()

        return 0

    lax.fori_loop(0, chunks, fetch, 0)
    q_copy.start()

    barrier = pltpu.get_barrier_semaphore()
    partners = [z_next, z_prev, base + sib] + [
        base + 2 * there + core for there in (beside, across, far)
    ]
    for partner in partners:
        pl.semaphore_signal(barrier, inc=1, device_id={"ctx": partner}, device_id_type=MESH)
    pl.semaphore_wait(barrier, len(partners))

    own_ids.wait()
    onward(ids_copy, 0)

    def start_own(chunk, _):
        for c in own_copies(chunk):
            c.wait()
        onward(copy, chunk)
        return 0

    lax.fori_loop(0, 1, start_own, 0)
    send_own(ids_copy, 0)
    send_own(copy, 0)
    lax.fori_loop(1, min(AHEAD + PAST + 1, chunks), start_own, 0)

    def ahead(chunk, _):
        send_own(copy, chunk)
        return 0

    lax.fori_loop(1, min(AHEAD + PAST, chunks), ahead, 0)

    def first(act, chunk):
        if chunk == 0:
            act(ids_copy, 0)
        if 0 <= chunk < chunks:
            act(copy, chunk)

    for turn in range(-PAST, 0):
        first(send_past, turn + PAST)
        first(relay_near, turn + NEAR)
        first(relay_far, turn + FAR)
    gather(ids_copy, 0)

    own_row = ids[0].astype(jnp.float32)
    query_ids = jnp.broadcast_to(own_row, (rows, rows)).T
    row = lax.broadcasted_iota(jnp.int32, (rows, rows), 0)
    column = lax.broadcasted_iota(jnp.int32, (rows, rows), 1)
    for steps in range(span, -1, -1):
        seen = query_ids == ids[steps].astype(jnp.float32)
        key_pos = (me - steps) * rows + column
        query_pos = me * rows + row
        seen = seen & (key_pos >= 0) & (key_pos <= query_pos)
        seen = seen & (query_pos - key_pos < VISIBLE_KEYS)
        bias[:, (span - steps) * rows : (span - steps + 1) * rows] = jnp.where(
            seen, jnp.float32(0.0), jnp.float32(-1e30)
        )
    q_copy.wait()
    factor = PRE_SCALAR ** (-0.5) * math.log2(math.e)

    def step(chunk, _):
        @pl.when(chunk + AHEAD + PAST + 1 < chunks)
        def _():
            start_own(chunk + AHEAD + PAST + 1, 0)

        for later, act in (
            (PAST + AHEAD, send_own),
            (PAST, send_past),
            (NEAR, relay_near),
        ):

            @pl.when(chunk + later < chunks)
            def _():
                act(copy, chunk + later)

        gather(copy, chunk)
        for head in range(CHUNK_HEADS):
            at = pl.multiple_of(chunk * cols + head * HEAD_SIZE, HEAD_SIZE)
            lanes = slice(head * HEAD_SIZE, (head + 1) * HEAD_SIZE)
            key_rows = kv[chunk, :, 0, :, lanes].reshape(keys, HEAD_SIZE)
            values = kv[chunk, :, 1, :, lanes].reshape(keys, HEAD_SIZE)
            weights, totals = [], []
            queries = jnp.concatenate(
                [
                    q_buf[:, pl.ds(pl.multiple_of(at * group + g * HEAD_SIZE, HEAD_SIZE), HEAD_SIZE)]
                    for g in range(group)
                ],
                axis=0,
            )
            scores = lax.dot_general(
                queries, key_rows, (((1,), (1,)), ((), ())), preferred_element_type=jnp.float32
            )
            for g in range(group):
                masked = scores[g * rows : (g + 1) * rows] + bias[...]
                top = jnp.max(masked, axis=1, keepdims=True)
                weight = jnp.exp2((masked - top) * factor)
                totals.append(jnp.sum(weight, axis=1, keepdims=True))
                weights.append(weight.astype(jnp.bfloat16))
            summed = jnp.dot(
                jnp.concatenate(weights, axis=0), values, preferred_element_type=jnp.float32
            )
            for g in range(group):
                to = pl.multiple_of(at * group + g * HEAD_SIZE, HEAD_SIZE)
                o_buf[:, pl.ds(to, HEAD_SIZE)] = (
                    summed[g * rows : (g + 1) * rows] / totals[g]
                ).astype(jnp.bfloat16)
        out_copy(chunk).start()

        @pl.when(chunk + FAR < chunks)
        def _():
            relay_far(copy, chunk + FAR)

        return 0

    lax.fori_loop(0, chunks, step, 0)

    def finish(chunk, _):
        sent(copy, chunk)
        out_copy(chunk).wait()
        return 0

    lax.fori_loop(0, chunks, finish, 0)
    sent(ids_copy, 0)


def per_device(n, rotated_queries, rotated_keys, projected_values, doc_ids):
    rows, q_width = rotated_queries.shape
    width = rotated_keys.shape[1]
    span = VISIBLE_KEYS // rows
    chunks = width // (CHUNK_HEADS * HEAD_SIZE)
    keys = VISIBLE_KEYS + rows
    dma = pltpu.SemaphoreType.DMA
    return pl.pallas_call(
        functools.partial(kernel, n, q_width // width),
        out_shape=jax.ShapeDtypeStruct((rows, q_width), jnp.bfloat16),
        in_specs=[pl.BlockSpec(memory_space=pl.ANY)] * 4,
        out_specs=pl.BlockSpec(memory_space=pl.ANY),
        scratch_shapes=[
            pltpu.VMEM((chunks, span + 1, 2, rows, width // chunks), jnp.bfloat16),
            pltpu.VMEM((span + 1, 1, rows), jnp.int32),
            pltpu.VMEM((rows, q_width), jnp.bfloat16),
            pltpu.VMEM((rows, q_width), jnp.bfloat16),
            pltpu.VMEM((rows, keys), jnp.float32),
            dma((10, chunks)),
            dma((span + 1, chunks)),
            dma((10,)),
            dma((span + 1,)),
            dma((2, chunks)),
            dma,
            dma,
            dma((chunks,)),
            dma((2, chunks)),
            dma,
        ],
        compiler_params=pltpu.CompilerParams(collective_id=0, has_side_effects=True),
    )(rotated_queries, rotated_keys, projected_values, doc_ids.reshape(1, rows))


def solution(mesh):
    in_specs = (P("ctx", "head"), P("ctx", "head"), P("ctx", "head"), P("ctx"))
    return jax.shard_map(
        functools.partial(per_device, mesh.shape["ctx"]),
        mesh=mesh,
        in_specs=in_specs,
        out_specs=P("ctx", "head"),
        check_vma=False,
    )
```

```python
import functools
import math

import jax
import jax.numpy as jnp
from jax import lax
from jax.experimental import pallas as pl
from jax.experimental.pallas import tpu as pltpu
from jax.sharding import PartitionSpec as P

HEAD_SIZE = 128
VISIBLE_KEYS = 1024
PRE_SCALAR = 168
CHUNK_HEADS = 1
AHEAD = 0
PAST = 7
NEAR = 4
FAR = 2
MESH = pl.DeviceIdType.MESH


def kernel(
    n,
    group,
    q_hbm,
    k_hbm,
    v_hbm,
    ids_hbm,
    o_hbm,
    kv,
    ids,
    q_buf,
    o_buf,
    bias,
    send_sem,
    recv_sem,
    ids_send_sem,
    ids_recv_sem,
    own_sem,
    q_sem,
    ids_sem,
    out_sem,
    stand_sem,
    ids_stand_sem,
):
    rows = q_hbm.shape[0]
    width = k_hbm.shape[1]
    span = VISIBLE_KEYS // rows
    keys = VISIBLE_KEYS + rows
    chips = span // 2
    cols = CHUNK_HEADS * HEAD_SIZE
    chunks = width // cols
    q_cols = cols * group
    me = lax.axis_index("ctx")
    local = lax.rem(me, span)
    base = me - local
    chip = local // 2
    core = lax.rem(local, 2)
    sib = 2 * chip + 1 - core
    z_next = lax.rem(me + span, n)
    z_prev = lax.rem(me + n - span, n)

    def back(dst, src):
        return lax.rem(dst - src + span, span)

    def block(steps, chunk):
        return kv.at[chunk, span - steps]

    def copy(src, dst, target, kind, chunk):
        return pltpu.make_async_remote_copy(
            src_ref=block(src, chunk),
            dst_ref=block(dst, chunk),
            send_sem=send_sem.at[kind, chunk],
            recv_sem=recv_sem.at[dst, chunk],
            device_id={"ctx": target},
            device_id_type=MESH,
        )

    def ids_copy(src, dst, target, kind, chunk):
        return pltpu.make_async_remote_copy(
            src_ref=ids.at[src],
            dst_ref=ids.at[dst],
            send_sem=ids_send_sem.at[kind],
            recv_sem=ids_recv_sem.at[dst],
            device_id={"ctx": target},
            device_id_type=MESH,
        )

    beside = chip + 1 - 2 * lax.rem(chip, 2)
    across = lax.rem(chip + 2, chips)
    far = 3 - chip

    def corner(source):
        return lax.rem(source, 3) == 0

    def by_across(source, chunk):
        third = lax.rem(chunk, 3)
        return jnp.logical_or(
            jnp.logical_and(corner(source), third == 1),
            jnp.logical_and(jnp.logical_not(corner(source)), third != 0),
        )

    def by_beside(source, chunk):
        return jnp.logical_and(corner(source), jnp.logical_not(by_across(source, chunk)))

    def straight(source, chunk):
        return jnp.logical_not(jnp.logical_or(corner(source), by_across(source, chunk)))

    def stand_in(chunk):
        start = pl.multiple_of(chunk * cols, cols)
        return [
            pltpu.make_async_copy(
                ref.at[:, pl.ds(start, cols)], kv.at[chunk, 0, which], stand_sem.at[which, chunk]
            )
            for which, ref in enumerate((k_hbm, v_hbm))
        ]

    ids_stand = pltpu.make_async_copy(ids_hbm, ids.at[span], ids_stand_sem)

    def onward(copy, chunk):
        @pl.when(me + span < n)
        def _():
            copy(0, span, z_next, 0, chunk).start()

    def past_here(copy, chunk):
        @pl.when(me >= span)
        def _():
            copy(0, span, z_next, 0, chunk).wait_recv()

        @pl.when(me < span)
        def _():
            for c in [ids_stand] if copy is ids_copy else stand_in(chunk):
                c.wait()

    def send(copy, chunk, steps, chosen):
        for kind, there in ((1, beside), (2, across), (3, far)):
            to = 2 * there + core
            wanted = chosen(to)
            if kind == 3:
                wanted = jnp.logical_and(wanted, straight(chip, chunk))

            @pl.when(wanted)
            def _():
                copy(steps, back(to, local), base + to, kind, chunk).start()

        @pl.when(chosen(sib))
        def _():
            copy(steps, back(sib, local), base + sib, 4, chunk).start()

    def send_own(copy, chunk):
        send(copy, chunk, 0, lambda to: to > local)

    def send_past(copy, chunk):
        past_here(copy, chunk)
        send(copy, chunk, span, lambda to: to < local)

    def to_sib(copy, chunk, there, kind):
        source = 2 * there + core
        copy(back(local, source), back(sib, source), base + sib, kind, chunk).start()

    def arrive(copy, chunk, there):
        copy(0, back(local, 2 * there + core), z_next, 0, chunk).wait_recv()

    def relay_near(copy, chunk):
        for kind, there, target, chosen in (
            (8, across, beside, by_across),
            (9, beside, across, by_beside),
        ):
            arrive(copy, chunk, there)
            source, to = 2 * there + core, 2 * target + core

            @pl.when(chosen(there, chunk))
            def _():
                copy(back(local, source), back(to, source), base + to, kind, chunk).start()

            to_sib(copy, chunk, there, kind - 3)

    def relay_far(copy, chunk):
        arrive(copy, chunk, far)
        to_sib(copy, chunk, far, 7)

    def gather(copy, chunk):
        copy(0, back(local, sib), z_next, 0, chunk).wait_recv()
        for there in (beside, across, far):
            copy(0, back(local, 2 * there + 1 - core), z_next, 0, chunk).wait_recv()

    def sent(copy, chunk):
        for kind in (1, 2, 4, 5, 6, 7):
            copy(0, span, z_next, kind, chunk).wait_send()
        for kind, wanted in (
            (0, me + span < n),
            (3, straight(chip, chunk)),
            (8, by_across(across, chunk)),
            (9, by_beside(beside, chunk)),
        ):

            @pl.when(wanted)
            def _():
                copy(0, span, z_next, kind, chunk).wait_send()

    def own_copies(chunk):
        start = pl.multiple_of(chunk * cols, cols)
        return [
            pltpu.make_async_copy(
                ref.at[:, pl.ds(start, cols)],
                kv.at[chunk, span, which],
                own_sem.at[which, chunk],
            )
            for which, ref in enumerate((k_hbm, v_hbm))
        ]

    q_copy = pltpu.make_async_copy(q_hbm, q_buf, q_sem)
    own_ids = pltpu.make_async_copy(ids_hbm, ids.at[0], ids_sem)

    def out_copy(chunk):
        part = pl.ds(pl.multiple_of(chunk * q_cols, q_cols), q_cols)
        return pltpu.make_async_copy(o_buf.at[:, part], o_hbm.at[:, part], out_sem.at[chunk])

    own_ids.start()

    @pl.when(me < span)
    def _():
        ids_stand.start()

    def fetch(chunk, _):
        for c in own_copies(chunk):
            c.start()

        @pl.when(me < span)
        def _():
            for c in stand_in(chunk):
                c.start()

        return 0

    lax.fori_loop(0, chunks, fetch, 0)
    q_copy.start()

    barrier = pltpu.get_barrier_semaphore()
    partners = [z_next, z_prev, base + sib] + [
        base + 2 * there + core for there in (beside, across, far)
    ]
    for partner in partners:
        pl.semaphore_signal(barrier, inc=1, device_id={"ctx": partner}, device_id_type=MESH)
    pl.semaphore_wait(barrier, len(partners))

    own_ids.wait()
    onward(ids_copy, 0)

    def start_own(chunk, _):
        for c in own_copies(chunk):
            c.wait()
        onward(copy, chunk)
        return 0

    lax.fori_loop(0, 1, start_own, 0)
    send_own(ids_copy, 0)
    send_own(copy, 0)
    lax.fori_loop(1, min(AHEAD + PAST + 1, chunks), start_own, 0)

    def ahead(chunk, _):
        send_own(copy, chunk)
        return 0

    lax.fori_loop(1, min(AHEAD + PAST, chunks), ahead, 0)

    def first(act, chunk):
        if chunk == 0:
            act(ids_copy, 0)
        if 0 <= chunk < chunks:
            act(copy, chunk)

    for turn in range(-PAST, 0):
        first(send_past, turn + PAST)
        first(relay_near, turn + NEAR)
        first(relay_far, turn + FAR)
    gather(ids_copy, 0)

    own_row = ids[0].astype(jnp.float32)
    query_ids = jnp.broadcast_to(own_row, (rows, rows)).T
    row = lax.broadcasted_iota(jnp.int32, (rows, rows), 0)
    column = lax.broadcasted_iota(jnp.int32, (rows, rows), 1)
    for steps in range(span, -1, -1):
        seen = query_ids == ids[steps].astype(jnp.float32)
        key_pos = (me - steps) * rows + column
        query_pos = me * rows + row
        seen = seen & (key_pos >= 0) & (key_pos <= query_pos)
        seen = seen & (query_pos - key_pos < VISIBLE_KEYS)
        bias[:, (span - steps) * rows : (span - steps + 1) * rows] = jnp.where(
            seen, jnp.float32(0.0), jnp.float32(-1e30)
        )
    q_copy.wait()
    factor = PRE_SCALAR ** (-0.5) * math.log2(math.e)

    def step(chunk, _):
        @pl.when(chunk + AHEAD + PAST + 1 < chunks)
        def _():
            start_own(chunk + AHEAD + PAST + 1, 0)

        for later, act in (
            (PAST + AHEAD, send_own),
            (PAST, send_past),
            (NEAR, relay_near),
        ):

            @pl.when(chunk + later < chunks)
            def _():
                act(copy, chunk + later)

        gather(copy, chunk)
        for head in range(CHUNK_HEADS):
            at = pl.multiple_of(chunk * cols + head * HEAD_SIZE, HEAD_SIZE)
            lanes = slice(head * HEAD_SIZE, (head + 1) * HEAD_SIZE)
            key_rows = kv[chunk, :, 0, :, lanes].reshape(keys, HEAD_SIZE)
            values = kv[chunk, :, 1, :, lanes].reshape(keys, HEAD_SIZE)
            weights, totals = [], []
            queries = jnp.concatenate(
                [
                    q_buf[:, pl.ds(pl.multiple_of(at * group + g * HEAD_SIZE, HEAD_SIZE), HEAD_SIZE)]
                    for g in range(group)
                ],
                axis=0,
            )
            scores = lax.dot_general(
                queries, key_rows, (((1,), (1,)), ((), ())), preferred_element_type=jnp.float32
            )
            for g in range(group):
                masked = scores[g * rows : (g + 1) * rows] + bias[...]
                top = jnp.max(masked, axis=1, keepdims=True)
                weight = jnp.exp2((masked - top) * factor)
                totals.append(jnp.sum(weight, axis=1, keepdims=True))
                weights.append(weight.astype(jnp.bfloat16))
            summed = jnp.dot(
                jnp.concatenate(weights, axis=0), values, preferred_element_type=jnp.float32
            )
            for g in range(group):
                to = pl.multiple_of(at * group + g * HEAD_SIZE, HEAD_SIZE)
                o_buf[:, pl.ds(to, HEAD_SIZE)] = (
                    summed[g * rows : (g + 1) * rows] / totals[g]
                ).astype(jnp.bfloat16)
        out_copy(chunk).start()

        @pl.when(chunk + FAR < chunks)
        def _():
            relay_far(copy, chunk + FAR)

        return 0

    lax.fori_loop(0, chunks, step, 0)

    def finish(chunk, _):
        sent(copy, chunk)
        out_copy(chunk).wait()
        return 0

    lax.fori_loop(0, chunks, finish, 0)
    sent(ids_copy, 0)


def per_device(n, rotated_queries, rotated_keys, projected_values, doc_ids):
    rows, q_width = rotated_queries.shape
    width = rotated_keys.shape[1]
    span = VISIBLE_KEYS // rows
    chunks = width // (CHUNK_HEADS * HEAD_SIZE)
    keys = VISIBLE_KEYS + rows
    dma = pltpu.SemaphoreType.DMA
    return pl.pallas_call(
        functools.partial(kernel, n, q_width // width),
        out_shape=jax.ShapeDtypeStruct((rows, q_width), jnp.bfloat16),
        in_specs=[pl.BlockSpec(memory_space=pl.ANY)] * 4,
        out_specs=pl.BlockSpec(memory_space=pl.ANY),
        scratch_shapes=[
            pltpu.VMEM((chunks, span + 1, 2, rows, width // chunks), jnp.bfloat16),
            pltpu.VMEM((span + 1, 1, rows), jnp.int32),
            pltpu.VMEM((rows, q_width), jnp.bfloat16),
            pltpu.VMEM((rows, q_width), jnp.bfloat16),
            pltpu.VMEM((rows, keys), jnp.float32),
            dma((10, chunks)),
            dma((span + 1, chunks)),
            dma((10,)),
            dma((span + 1,)),
            dma((2, chunks)),
            dma,
            dma,
            dma((chunks,)),
            dma((2, chunks)),
            dma,
        ],
        compiler_params=pltpu.CompilerParams(collective_id=0, has_side_effects=True),
    )(rotated_queries, rotated_keys, projected_values, doc_ids.reshape(1, rows))


def solution(mesh):
    in_specs = (P("ctx", "head"), P("ctx", "head"), P("ctx", "head"), P("ctx"))
    return jax.shard_map(
        functools.partial(per_device, mesh.shape["ctx"]),
        mesh=mesh,
        in_specs=in_specs,
        out_specs=P("ctx", "head"),
        check_vma=False,
    )
```
